128 devices in a mesh: dp: 32 (over z, x, core), tensor: 4 (over y).
Axes of the slice: x: 4, y: 4, z: 4, core: 2. Of those that a mesh axis runs over, the one named last changes fastest.
Arguments:
- activations: bfloat16 [4, 16384, 14336], P(None, 'dp', 'tensor'), may hold values from -6 to 6
- out_grads: bfloat16 [4, 16384, 4096], P(None, 'dp', 'tensor'), may hold values from -6 to 6
- proj_in: bfloat16 [4, 40, 14336], P(None, None, 'tensor'), may hold values from -0.046875 to 0.046875
- proj_out: bfloat16 [4, 40, 4096], P(None, None, 'tensor'), may hold values from -0.09375 to 0.09375
- lengths: int32 [128], P('dp'), may hold values from 16 to 128
- example_ids: int32 [128], P('dp'), may hold values from 0 to 127, each once
- prior_cov: bfloat16 [4, 1600, 1600], P('tensor'), as said below
- damping: float32 [4], P('tensor'), may hold values from 10 to 100
- queries: float32 [4, 64, 1600], P('tensor'), may hold values from -2 to 2
Outputs:
- scores: float32 [128, 64], P('dp')
The draws below stay inside these ranges and needn't reach their ends.
Inputs may be any that keep to these rules, and one draw needn't show every extreme that they name: Each slot's tokens at positions from lengths on are padding. `example_ids`: a permutation of the examples over the slots. `prior_cov`: symmetric and positive definite.
All inputs are finite; a program needn't handle non-finite values.
Results may differ from the reference program's by a relative error of at most 0.0003.
Values sent between devices are 32-bit elements; how exact they have to be, the bound alone decides.
No kernel may reach another device: no remote copies, remote signals or barrier semaphores. Data moves between devices by JAX's collectives and lax.ppermute only.
A program may use at most 128 MiB of HBM per device.

```python
import math
import jax
import jax.numpy as jnp
from jax import lax

D = 4096
FF = 14336
KP = 40
SEQ = 128
NQ = 64
PROJ = 1600
LAYERS = 4
EXAMPLES = 128
TOKENS = 16384


def draw_prior_cov(key, part):
    spread = 120.0 / PROJ

    def one_layer(layer_key):
        raw_values = jax.random.uniform(layer_key, (PROJ, PROJ), jnp.float32, -spread, spread)
        symmetric = 0.5 * (raw_values + raw_values.T)
        identity = jnp.eye(PROJ, dtype=jnp.float32)
        off_diag = symmetric * (1.0 - identity)
        row_abs = jnp.sum(jnp.abs(off_diag), axis=1)
        return (off_diag + identity * (1.5 * row_abs[:, None] + 1.0)).astype(jnp.bfloat16)
    layer_keys = jax.random.split(jax.random.fold_in(key, 17), LAYERS)
    return jax.vmap(one_layer)(layer_keys)


def with_ends(values, rng, least, top_value):
    spot = [jax.random.randint(jax.random.fold_in(rng, axis), (), 0, length) for axis, length in enumerate(values.shape)]
    widest = values.shape.index(max(values.shape))
    neighbour = spot[:widest] + [(spot[widest] + 1) % values.shape[widest]] + spot[widest + 1:]
    return values.at[tuple(spot)].set(least).at[tuple(neighbour)].set(top_value)


def block_scale(own_key, shape, cuts, low, high):
    loudness = 1.0
    for position, parts in cuts:
        heights = jax.random.uniform(jax.random.fold_in(jax.random.fold_in(own_key, 6), position), (parts,), jnp.float32, low / len(cuts), high / len(cuts))
        loudness = loudness * jnp.repeat(jnp.exp(heights), shape[position] // parts).reshape((-1,) + (1,) * (len(shape) - 1 - position))
    return loudness


def bell_draw(rng, shape, deviation, reach, pieces=(), held_as=jnp.bfloat16):
    values = deviation * jax.random.normal(rng, shape, jnp.float32)
    if pieces:
        values = values * block_scale(rng, shape, pieces, -0.22, 0.18)
    return jnp.clip(values, -reach, reach).astype(held_as)


def setup_inputs(seed: int = 0) -> dict:
    key_list = jax.random.split(jax.random.key(seed), 10)
    activations = bell_draw(key_list[0], (LAYERS, TOKENS, FF), 1.0, 6.0, ((1, 32), (2, 4)))
    out_grads = bell_draw(key_list[1], (LAYERS, TOKENS, D), 1.0, 6.0, ((1, 32), (2, 4)))
    proj_in = bell_draw(key_list[2], (LAYERS, KP, FF), FF ** -0.5, 0.046875, ((2, 4),))
    proj_out = bell_draw(key_list[3], (LAYERS, KP, D), D ** -0.5, 0.09375, ((2, 4),))
    lengths = with_ends(jax.random.randint(key_list[4], (EXAMPLES,), SEQ // 8, SEQ + 1), jax.random.fold_in(key_list[4], 1), SEQ // 8, SEQ).astype(jnp.int32)
    example_ids = jax.random.permutation(key_list[5], EXAMPLES).astype(jnp.int32)
    prior_cov = draw_prior_cov(jax.random.fold_in(key_list[9], 71), 0)
    damping = jnp.clip(jnp.exp(math.log(100.0) - 2.3025851 * jax.random.uniform(key_list[7], (LAYERS,), jnp.float32) ** block_scale(key_list[7], (LAYERS,), ((0, 4),), -0.2, 0.2)), 10.0, 100.0)
    queries = bell_draw(key_list[8], (LAYERS, NQ, PROJ), 0.3, 2.0, ((0, 4),), jnp.float32)
    return dict(activations=activations, out_grads=out_grads, proj_in=proj_in, proj_out=proj_out, lengths=lengths, example_ids=example_ids, prior_cov=prior_cov, damping=damping, queries=queries)


def reference(activations, out_grads, proj_in, proj_out, lengths, example_ids, prior_cov, damping, queries):
    live_mask = (jnp.arange(SEQ, dtype=jnp.int32)[None, :] < lengths[:, None]).astype(jnp.float32)
    slot_scores = jnp.zeros((EXAMPLES, NQ), jnp.float32)
    for layer_index in range(LAYERS):
        in_rows = jnp.dot(activations[layer_index].astype(jnp.float32), proj_in[layer_index].T.astype(jnp.float32), preferred_element_type=jnp.float32)
        out_rows = jnp.dot(out_grads[layer_index].astype(jnp.float32), proj_out[layer_index].T.astype(jnp.float32), preferred_element_type=jnp.float32)
        in_rows = in_rows.reshape(EXAMPLES, SEQ, KP) * live_mask[:, :, None]
        out_rows = out_rows.reshape(EXAMPLES, SEQ, KP)
        proj_grads = jnp.einsum('est,esu->etu', out_rows, in_rows, precision=lax.Precision.HIGHEST).reshape(EXAMPLES, PROJ)
        moment = jnp.dot(proj_grads.T, proj_grads, precision=lax.Precision.HIGHEST)
        covariance = prior_cov[layer_index].astype(jnp.float32) + moment / EXAMPLES + damping[layer_index] * jnp.eye(PROJ, dtype=jnp.float32)
        factor_lower = jnp.linalg.cholesky(covariance)
        forward_part = lax.linalg.triangular_solve(factor_lower, queries[layer_index].T, left_side=True, lower=True)
        solved = lax.linalg.triangular_solve(factor_lower, forward_part, left_side=True, lower=True, transpose_a=True)
        slot_scores = slot_scores + jnp.dot(proj_grads, solved, precision=lax.Precision.HIGHEST)
    return jnp.zeros((EXAMPLES, NQ), jnp.float32).at[example_ids].set(slot_scores)
```

```python
import jax
import jax.numpy as jnp
from jax import lax
from jax.experimental import pallas as pl
from jax.experimental.pallas import tpu as pltpu
from jax.sharding import PartitionSpec as P

KP = 40
B = 128


def split(x):
    high = x.astype(jnp.bfloat16)
    low = (x - high.astype(jnp.float32)).astype(jnp.bfloat16)
    return high, low


def down(row):
    return jnp.broadcast_to(row, (8, B))


def block_inverse(rows):
    lane = lax.broadcasted_iota(jnp.int32, (8, B), 1)
    sub = lax.broadcasted_iota(jnp.int32, (8, B), 0)
    rows = list(rows)
    for g in range(16):
        first = 8 * g
        columns = [
            [jnp.broadcast_to(rows[h][:, first + m : first + m + 1], (8, B)) for m in range(8)]
            for h in range(16)
        ]
        pivots = columns[g]
        in_pivot = (lane >= first) & (lane < first + 8)
        panel = jnp.where(in_pivot, jnp.where(lane - first == sub, 1.0, 0.0), rows[g])
        for j in range(8):
            r = down((1.0 / pivots[j])[j : j + 1])
            others = jnp.where(sub == j, 0.0, pivots[j])
            scaled = down(panel[j : j + 1]) * r
            panel = jnp.where(sub == j, scaled, panel) - others * scaled
            for m in range(j + 1, 8):
                scaled = down(pivots[m][j : j + 1]) * r
                pivots[m] = jnp.where(sub == j, scaled, pivots[m]) - others * scaled
        spread = [down(panel[m : m + 1]) for m in range(8)]
        for h in [(g + 1 + t) % 16 for t in range(15)]:
            total = columns[h][0] * spread[0]
            for m in range(1, 8):
                total = total + columns[h][m] * spread[m]
            rows[h] = jnp.where(in_pivot, 0.0, rows[h]) - total
        rows[g] = panel
    return rows


def solve_kernel(prior_ref, damp_ref, grads_ref, right_ref, out_ref, work, terms, inverse):
    size = prior_ref.shape[0]
    blocks = pl.cdiv(size, B)
    width = (blocks + 1) * B
    tail = blocks * B
    examples = grads_ref.shape[0]
    work[...] = jnp.zeros((width, width), jnp.float32)
    work[0:size, 0:size] = prior_ref[...].astype(jnp.float32)
    work[tail:width, 0:size] = right_ref[...]
    work[0:size, tail:width] = right_ref[...].T
    r = lax.broadcasted_iota(jnp.int32, (B, B), 0)
    c = lax.broadcasted_iota(jnp.int32, (B, B), 1)
    for k in range(blocks):
        here = slice(k * B, (k + 1) * B)
        work[here, here] += jnp.where(r == c, jnp.where(r + k * B < size, damp_ref[0], 1.0), 0.0)

    def set_terms(x, at):
        high, low = split(x)
        to = at + x.shape[1]
        terms[0:B, at:to] = high
        terms[B : 2 * B, at:to] = low
        terms[2 * B : 3 * B, at:to] = high

    def product(left, at):
        high, low = split(left)
        left = jnp.concatenate([high, high, low], axis=1)
        return jnp.dot(left, terms[:, at:], preferred_element_type=jnp.float32)

    terms[...] = jnp.zeros_like(terms)
    set_terms(grads_ref[...] * (1.0 / examples), 0)
    grads_t = grads_ref[...].T
    for k in range(blocks):
        here = slice(k * B, min((k + 1) * B, size))
        work[here, :] += product(grads_t[here], 0)

    def eliminate(k, at):
        first = pl.multiple_of(k * B, B)
        block = work[pl.ds(first, B), pl.ds(first, B)]
        for h, piece in enumerate(block_inverse([block[8 * h : 8 * h + 8] for h in range(16)])):
            inverse[8 * h : 8 * h + 8] = piece
        panel = jnp.dot(
            inverse[...],
            work[pl.ds(first, B), at:],
            preferred_element_type=jnp.float32,
            precision=lax.Precision.HIGHEST,
        )
        set_terms(panel, at)

        def update(i, carry):
            rows = pl.ds(pl.multiple_of(i * B, B), B)
            work[rows, at:] -= product(work[rows, pl.ds(first, B)], at)
            return carry

        lax.fori_loop(k + 1, blocks + 1, update, 0)

    starts = (0, 4, 8)
    for start, stop in zip(starts, (*starts[1:], blocks)):

        def body(k, carry, at=start * B):
            eliminate(k, at)
            return carry

        lax.fori_loop(start, stop, body, 0)
    out_ref[...] = -work[tail:width, tail:width]


def scores_of(prior, damping, grads, right):
    width = (pl.cdiv(prior.shape[0], B) + 1) * B
    vmem = pl.BlockSpec(memory_space=pltpu.VMEM)
    return pl.pallas_call(
        solve_kernel,
        out_shape=jax.ShapeDtypeStruct((B, B), jnp.float32),
        in_specs=[vmem, pl.BlockSpec(memory_space=pltpu.SMEM), vmem, vmem],
        out_specs=vmem,
        scratch_shapes=[
            pltpu.VMEM((width, width), jnp.float32),
            pltpu.VMEM((3 * B, width), jnp.bfloat16),
            pltpu.VMEM((B, B), jnp.float32),
        ],
        compiler_params=pltpu.CompilerParams(vmem_limit_bytes=60 * 2**20),
    )(prior, damping, grads, right)


def cut_along(x, dim, length):
    dims = x.shape
    pieces = x.reshape(*dims[:dim], length, dims[dim] // length, *dims[dim + 1 :])
    return jnp.moveaxis(pieces, dim, 0)


def sent_and_summed(x, axis, dim):
    length = lax.axis_size(axis)
    pieces = lax.all_to_all(cut_along(x, dim, length), axis, 0, 0, tiled=True)
    return jnp.sum(pieces, axis=0)


def per_device(
    activations, out_grads, proj_in, proj_out, lengths, example_ids, prior_cov, damping, queries
):
    ex_local = lengths.shape[0]
    seq_len = activations.shape[1] // ex_local
    tokens = activations.shape[1]
    proj_size = KP * KP
    n_query = queries.shape[1]
    live_mask = (jnp.arange(seq_len, dtype=jnp.int32)[None, :] < lengths[:, None]).astype(
        jnp.float32
    )
    in_parts = jnp.einsum("ltf,lkf->ltk", activations, proj_in, preferred_element_type=jnp.float32)
    out_parts = jnp.einsum("ltf,lkf->ltk", out_grads, proj_out, preferred_element_type=jnp.float32)
    owned = sent_and_summed(jnp.concatenate([in_parts, out_parts], axis=1), "tensor", 0)[0]
    in_rows = owned[:tokens].reshape(ex_local, seq_len, KP) * live_mask[:, :, None]
    out_rows = owned[tokens:].reshape(ex_local, seq_len, KP)
    proj_grads = jnp.einsum(
        "est,esu->etu", out_rows, in_rows, precision=lax.Precision.HIGHEST
    ).reshape(ex_local, proj_size)
    sent = jnp.concatenate([proj_grads, example_ids.astype(jnp.float32)[:, None]], axis=1)
    gathered = lax.all_gather(sent, "dp", axis=0, tiled=True)
    grads = gathered[:, :proj_size]
    ids = gathered[:, proj_size].astype(jnp.int32)
    mine = lax.axis_index("dp") * ex_local + jnp.arange(ex_local, dtype=jnp.int32)
    pick = (ids[None, :] == mine[:, None]).astype(jnp.float32)
    picked = jnp.dot(pick, grads, precision=lax.Precision.HIGHEST)
    right = jnp.concatenate(
        [queries[0], picked, jnp.zeros((B - n_query - ex_local, proj_size), jnp.float32)], axis=0
    )
    product = scores_of(prior_cov[0], damping, grads, right)
    layer_scores = product[n_query : n_query + ex_local, :n_query]
    return lax.psum(layer_scores, "tensor")


def solution(mesh):
    in_specs = (
        P(None, "dp", "tensor"),
        P(None, "dp", "tensor"),
        P(None, None, "tensor"),
        P(None, None, "tensor"),
        P("dp"),
        P("dp"),
        P("tensor", None, None),
        P("tensor"),
        P("tensor", None, None),
    )
    out_specs = P("dp", None)
    return jax.shard_map(
        per_device, mesh=mesh, in_specs=in_specs, out_specs=out_specs, check_vma=False
    )
```

```python
import jax
import jax.numpy as jnp
from jax import lax
from jax.experimental import pallas as pl
from jax.experimental.pallas import tpu as pltpu
from jax.sharding import PartitionSpec as P

KP = 40
B = 128
S = 16
STARTS = (0, 3, 6, 9)


def split(x):
    high = x.astype(jnp.bfloat16)
    low = (x - high.astype(jnp.float32)).astype(jnp.bfloat16)
    return high, low


def down(row):
    return jnp.broadcast_to(row, (8, B))


def block_inverse(block):
    lane = lax.broadcasted_iota(jnp.int32, (8, B), 1)
    sub = lax.broadcasted_iota(jnp.int32, (8, B), 0)
    rows = [block[8 * h : 8 * h + 8] for h in range(16)]

    def columns(piece, first):
        return [jnp.broadcast_to(piece[:, first + m : first + m + 1], (8, B)) for m in range(S)]

    for g in range(B // S):
        first = S * g
        here = (2 * g, 2 * g + 1)
        in_pivot = (lane >= first) & (lane < first + S)
        cols = [list(pair) for pair in zip(*(columns(rows[h], first) for h in here))]
        after = (2 * g + 2, 2 * g + 3) if g + 1 < B // S else ()
        next_cols = [columns(rows[h], first) for h in after]
        panel = [
            jnp.where(in_pivot, jnp.where(lane - first == sub + 8 * q, 1.0, 0.0), rows[h])
            for q, h in enumerate(here)
        ]
        for j in range(S):
            a, s = j // 8, j % 8
            pivot = cols[j]
            r = down((1.0 / pivot[a])[s : s + 1])
            others = jnp.where(sub == s, 0.0, pivot[a])
            for item in (*cols[j + 1 :], panel):
                scaled = down(item[a][s : s + 1]) * r
                item[a] = jnp.where(sub == s, scaled, item[a]) - others * scaled
                item[1 - a] = item[1 - a] - pivot[1 - a] * scaled
        high, low = split(jnp.concatenate(panel, axis=0))
        both = jnp.concatenate([high, low], axis=1)
        parts = [jnp.zeros((S, 2 * B), jnp.bfloat16)] * (B // S)
        parts[g] = both
        right = jnp.concatenate(parts + parts, axis=0)
        left = jnp.concatenate(split(jnp.concatenate(rows, axis=0)), axis=1)
        change = jnp.dot(left, right, preferred_element_type=jnp.float32)
        change = change[:, :B] + change[:, B:]
        fresh = []
        for h in range(16):
            if h in here:
                fresh.append(panel[h - here[0]])
                continue
            kept = jnp.where(in_pivot, 0.0, rows[h])
            if h in after:
                terms = [
                    c * down(panel[m // 8][m % 8 : m % 8 + 1])
                    for m, c in enumerate(next_cols[h - after[0]])
                ]
                while len(terms) > 1:
                    terms = [x + y for x, y in zip(terms[::2], terms[1::2])]
                fresh.append(kept - terms[0])
            else:
                fresh.append(kept - change[8 * h : 8 * h + 8])
        rows = fresh
    return jnp.concatenate(rows, axis=0)


def solve_kernel(prior_ref, damp_ref, grads_ref, right_ref, out_ref, work, left, terms):
    size = prior_ref.shape[0]
    blocks = pl.cdiv(size, B)
    tail = blocks * B
    examples = grads_ref.shape[0]
    whole = size // B * B
    r = lax.broadcasted_iota(jnp.int32, (B, B), 0)
    c = lax.broadcasted_iota(jnp.int32, (B, B), 1)

    def set_left(rows, x):
        high, low = split(x)
        left[rows, 0:B] = high
        left[rows, B : 2 * B] = high
        left[rows, 2 * B :] = low

    def set_terms(rows, x):
        high, low = split(x)
        terms[rows, 0:B] = high
        terms[rows, B : 2 * B] = low
        terms[rows, 2 * B :] = high

    for k in range(blocks):
        here = slice(k * B, min((k + 1) * B, size))
        work[here, 0 : here.stop] = prior_ref[here, 0 : here.stop].astype(jnp.float32)
        if here.stop < (k + 1) * B:
            work[here.stop : (k + 1) * B, 0 : (k + 1) * B] = jnp.zeros(((k + 1) * B - size, (k + 1) * B), jnp.float32)
            work[here, here.stop : (k + 1) * B] = jnp.zeros((size - k * B, (k + 1) * B - size), jnp.float32)
        spot = slice(k * B, (k + 1) * B)
        work[spot, spot] += jnp.where(r == c, jnp.where(r + k * B < size, damp_ref[0], 1.0), 0.0)
    work[tail : tail + B, 0:size] = right_ref[...]
    work[tail : tail + B, size:tail] = jnp.zeros((B, tail - size), jnp.float32)
    work[tail : tail + B, tail : tail + B] = jnp.zeros((B, B), jnp.float32)
    left[...] = jnp.zeros_like(left)
    terms[...] = jnp.zeros_like(terms)
    grads_t = grads_ref[...].T
    set_left(slice(0, size), grads_t)
    set_terms(slice(0, size), grads_t * (-1.0 / examples))

    def product(x, y):
        return lax.dot_general(x, y, (((1,), (1,)), ((), ())), preferred_element_type=jnp.float32)

    def step(k, count):
        def at(t, n=1):
            return pl.ds(pl.multiple_of((k + t) * B, B), n * B)

        inverse = block_inverse(work[at(0), at(0)] - product(left[at(0), :], terms[at(0), :]))
        for t in range(0, count, 2):
            n = min(2, count - t)
            rows = at(t, count - t)
            work[rows, at(t, n)] -= product(left[rows, :], terms[at(t, n), :])
        rows = at(1, count - 1)
        set_left(rows, work[rows, at(0)])
        high, low = split(inverse)
        stacked = jnp.concatenate([high, low, high], axis=0)
        set_terms(rows, jnp.dot(left[rows, :], stacked, preferred_element_type=jnp.float32))

    for start, stop in zip(STARTS, (*STARTS[1:], blocks)):

        def body(k, carry, count=blocks + 1 - start):
            step(k, count)
            return carry

        lax.fori_loop(start, stop, body, 0)
    last = slice(tail, tail + B)
    out_ref[...] = product(left[last, :], terms[last, :]) - work[last, last]


def scores_of(prior, damping, grads, right):
    blocks = pl.cdiv(prior.shape[0], B)
    most = max(b - a for a, b in zip(STARTS, (*STARTS[1:], blocks)))
    width = (blocks + most) * B
    vmem = pl.BlockSpec(memory_space=pltpu.VMEM)
    return pl.pallas_call(
        solve_kernel,
        out_shape=jax.ShapeDtypeStruct((B, B), jnp.float32),
        in_specs=[vmem, pl.BlockSpec(memory_space=pltpu.SMEM), vmem, vmem],
        out_specs=vmem,
        scratch_shapes=[
            pltpu.VMEM((width, width), jnp.float32),
            pltpu.VMEM((width, 3 * B), jnp.bfloat16),
            pltpu.VMEM((width, 3 * B), jnp.bfloat16),
        ],
        compiler_params=pltpu.CompilerParams(vmem_limit_bytes=60 * 2**20),
    )(prior, damping, grads, right)


def to_layer(parts, axis):
    length = lax.axis_size(axis)
    me = lax.axis_index(axis)
    total = lax.dynamic_index_in_dim(parts, me, 0, keepdims=False)
    for d in (1, length - 1, *range(2, length - 1)):
        piece = lax.dynamic_index_in_dim(parts, lax.rem(me + d, length), 0, keepdims=False)
        total = total + lax.ppermute(piece, axis, [(i, (i + d) % length) for i in range(length)])
    return total


def gather_pairs(x, axis):
    length = lax.axis_size(axis)
    chips = length // 2
    groups = [[2 * i + c for i in range(chips)] for c in range(2)]
    spread = jnp.broadcast_to(x[None], (chips, *x.shape))
    mine = lax.all_to_all(spread, axis, 0, 0, axis_index_groups=groups, tiled=True)
    theirs = lax.ppermute(mine, axis, [(i, i ^ 1) for i in range(length)])
    first = lax.rem(lax.axis_index(axis), 2) == 0
    pairs = jnp.stack([jnp.where(first, mine, theirs), jnp.where(first, theirs, mine)], axis=1)
    return pairs.reshape(length * x.shape[0], *x.shape[1:])


def sum_of_four(x, axis):
    other = [lax.ppermute(x, axis, [(i, i ^ d) for i in range(4)]) for d in (1, 2, 3)]
    return (x + other[0]) + (other[1] + other[2])


def per_device(
    activations, out_grads, proj_in, proj_out, lengths, example_ids, prior_cov, damping, queries
):
    ex_local = lengths.shape[0]
    seq_len = activations.shape[1] // ex_local
    tokens = activations.shape[1]
    proj_size = KP * KP
    n_query = queries.shape[1]
    live_mask = (jnp.arange(seq_len, dtype=jnp.int32)[None, :] < lengths[:, None]).astype(
        jnp.float32
    )
    in_parts = jnp.einsum("ltf,lkf->ltk", activations, proj_in, preferred_element_type=jnp.float32)
    out_parts = jnp.einsum("ltf,lkf->ltk", out_grads, proj_out, preferred_element_type=jnp.float32)
    owned = to_layer(jnp.concatenate([in_parts, out_parts], axis=1), "tensor")
    in_rows = owned[:tokens].reshape(ex_local, seq_len, KP) * live_mask[:, :, None]
    out_rows = owned[tokens:].reshape(ex_local, seq_len, KP)
    proj_grads = jnp.einsum(
        "est,esu->etu", out_rows, in_rows, precision=lax.Precision.HIGHEST
    ).reshape(ex_local, proj_size)
    sent = jnp.concatenate([proj_grads, example_ids.astype(jnp.float32)[:, None]], axis=1)
    gathered = gather_pairs(sent, "dp")
    grads = gathered[:, :proj_size]
    ids = gathered[:, proj_size].astype(jnp.int32)
    mine = lax.axis_index("dp") * ex_local + jnp.arange(ex_local, dtype=jnp.int32)
    pick = (ids[None, :] == mine[:, None]).astype(jnp.float32)
    picked = jnp.dot(pick, grads, precision=lax.Precision.HIGHEST)
    right = jnp.concatenate(
        [queries[0], picked, jnp.zeros((B - n_query - ex_local, proj_size), jnp.float32)], axis=0
    )
    product = scores_of(prior_cov[0], damping, grads, right)
    layer_scores = product[n_query : n_query + ex_local, :n_query]
    return sum_of_four(layer_scores, "tensor")


def solution(mesh):
    in_specs = (
        P(None, "dp", "tensor"),
        P(None, "dp", "tensor"),
        P(None, None, "tensor"),
        P(None, None, "tensor"),
        P("dp"),
        P("dp"),
        P("tensor", None, None),
        P("tensor"),
        P("tensor", None, None),
    )
    out_specs = P("dp", None)
    return jax.shard_map(
        per_device, mesh=mesh, in_specs=in_specs, out_specs=out_specs, check_vma=False
    )
```

```python
import jax
import jax.numpy as jnp
from jax import lax
from jax.experimental import pallas as pl
from jax.experimental.pallas import tpu as pltpu
from jax.sharding import PartitionSpec as P

KP = 40
B = 128
S = 16
STARTS = (0, 3, 6, 9)


def split(x):
    high = x.astype(jnp.bfloat16)
    low = (x - high.astype(jnp.float32)).astype(jnp.bfloat16)
    return high, low


def down(row):
    return jnp.broadcast_to(row, (8, B))


def block_inverse(block, groups, beside):
    lane = lax.broadcasted_iota(jnp.int32, (8, B), 1)
    sub = lax.broadcasted_iota(jnp.int32, (8, B), 0)
    rows = [block[8 * h : 8 * h + 8] for h in range(16)]

    def columns(piece, first):
        return [jnp.broadcast_to(piece[:, first + m : first + m + 1], (8, B)) for m in range(S)]

    for g in range(groups):
        first = S * g
        here = (2 * g, 2 * g + 1)
        in_pivot = (lane >= first) & (lane < first + S)
        cols = [list(pair) for pair in zip(*(columns(rows[h], first) for h in here))]
        after = (2 * g + 2, 2 * g + 3) if g + 1 < groups else ()
        next_cols = [columns(rows[h], first) for h in after]
        panel = [
            jnp.where(in_pivot, jnp.where(lane - first == sub + 8 * q, 1.0, 0.0), rows[h])
            for q, h in enumerate(here)
        ]
        for j in range(S):
            a, s = j // 8, j % 8
            pivot = cols[j]
            r = down((1.0 / pivot[a])[s : s + 1])
            others = jnp.where(sub == s, 0.0, pivot[a])
            for item in (*cols[j + 1 :], panel):
                scaled = down(item[a][s : s + 1]) * r
                item[a] = jnp.where(sub == s, scaled, item[a]) - others * scaled
                item[1 - a] = item[1 - a] - pivot[1 - a] * scaled
        high, low = split(jnp.concatenate(panel, axis=0))
        both = jnp.concatenate([high, low], axis=1)
        parts = [jnp.zeros((S, 2 * B), jnp.bfloat16)] * (B // S)
        parts[g] = both
        right = jnp.concatenate(parts + parts, axis=0)
        left = jnp.concatenate(split(jnp.concatenate(rows, axis=0)), axis=1)
        change = jnp.dot(left, right, preferred_element_type=jnp.float32)
        change = change[:, :B] + change[:, B:]
        fresh = []
        for h in range(16):
            if h in here:
                fresh.append(panel[h - here[0]])
                continue
            kept = jnp.where(in_pivot, 0.0, rows[h])
            if h in after:
                terms = [
                    c * down(panel[m // 8][m % 8 : m % 8 + 1])
                    for m, c in enumerate(next_cols[h - after[0]])
                ]
                while len(terms) > 1:
                    terms = [x + y for x, y in zip(terms[::2], terms[1::2])]
                fresh.append(kept - terms[0])
            else:
                fresh.append(kept - change[8 * h : 8 * h + 8])
        rows = fresh
        beside(g)
    return jnp.concatenate(rows, axis=0)


def solve_kernel(prior_ref, damp_ref, first_ref, slots_ref, queries_ref, out_ref, work, left, terms):
    size = prior_ref.shape[0]
    blocks = pl.cdiv(size, B)
    tail = blocks * B
    examples = slots_ref.shape[0]
    n_query = queries_ref.shape[0]
    n_own = out_ref.shape[0]
    whole = size // B * B
    r = lax.broadcasted_iota(jnp.int32, (B, B), 0)
    c = lax.broadcasted_iota(jnp.int32, (B, B), 1)

    def set_left(rows, x):
        high, low = split(x)
        left[rows, 0:B] = high
        left[rows, B : 2 * B] = high
        left[rows, 2 * B :] = low

    def set_terms(rows, x):
        high, low = split(x)
        terms[rows, 0:B] = high
        terms[rows, B : 2 * B] = low
        terms[rows, 2 * B :] = high

    for k in range(blocks):
        here = slice(k * B, min((k + 1) * B, size))
        work[here, 0 : here.stop] = prior_ref[here, 0 : here.stop].astype(jnp.float32)
        if here.stop < (k + 1) * B:
            work[here.stop : (k + 1) * B, 0 : (k + 1) * B] = jnp.zeros(((k + 1) * B - size, (k + 1) * B), jnp.float32)
            work[here, here.stop : (k + 1) * B] = jnp.zeros((size - k * B, (k + 1) * B - size), jnp.float32)
        spot = slice(k * B, (k + 1) * B)
        work[spot, spot] += jnp.where(r == c, jnp.where(r + k * B < size, damp_ref[0], 1.0), 0.0)
    slots = jnp.concatenate(
        [slots_ref[...], jnp.zeros((examples, tail - slots_ref.shape[1]), jnp.float32)], axis=1
    )
    slots_t = slots.T
    grads = slots[:, :size]
    grads_t = slots_t[:size]
    ids = jnp.broadcast_to(slots_t[size : size + 1].astype(jnp.int32), (B - n_query, examples))
    row = lax.broadcasted_iota(jnp.int32, (B - n_query, examples), 0)
    pick = jnp.where((ids == row + first_ref[0]) & (row < n_own), 1.0, 0.0)
    work[tail : tail + n_query, 0:size] = queries_ref[...]
    work[tail + n_query : tail + B, 0:size] = jnp.dot(
        pick, grads, preferred_element_type=jnp.float32, precision=lax.Precision.HIGHEST
    )
    work[tail : tail + B, size:tail] = jnp.zeros((B, tail - size), jnp.float32)
    work[tail : tail + B, tail : tail + B] = jnp.zeros((B, B), jnp.float32)
    for ref in (left, terms):
        ref[size:, :] = jnp.zeros((ref.shape[0] - size, ref.shape[1]), ref.dtype)
    set_left(slice(0, size), grads_t)
    set_terms(slice(0, size), grads_t * (-1.0 / examples))

    def product(x, y):
        return lax.dot_general(x, y, (((1,), (1,)), ((), ())), preferred_element_type=jnp.float32)

    def step(k, count, groups):
        def at(t, n=1):
            return pl.ds(pl.multiple_of((k + t) * B, B), n * B)

        def beside(g):
            t = 2 * g
            if t < count:
                n = min(2, count - t)
                rows = at(t, count - t)
                work[rows, at(t, n)] -= product(left[rows, :], terms[at(t, n), :])

        block = work[at(0), at(0)] - product(left[at(0), :], terms[at(0), :])
        inverse = block_inverse(block, groups, beside)
        rows = at(1, count - 1)
        set_left(rows, work[rows, at(0)])
        high, low = split(inverse)
        stacked = jnp.concatenate([high, low, high], axis=0)
        set_terms(rows, jnp.dot(left[rows, :], stacked, preferred_element_type=jnp.float32))

    for start, stop in zip(STARTS, (*STARTS[1:], blocks - 1)):

        def body(k, carry, count=blocks + 1 - start):
            step(k, count, B // S)
            return carry

        lax.fori_loop(start, stop, body, 0)
    step(blocks - 1, 2, pl.cdiv(size - (blocks - 1) * B, S))
    last = slice(tail, tail + B)
    result = product(left[last, :], terms[last, :]) - work[last, last]
    out_ref[...] = result[n_query : n_query + n_own, :n_query]


def scores_of(prior, damping, first, slots, queries, own):
    blocks = pl.cdiv(prior.shape[0], B)
    most = max(b - a for a, b in zip(STARTS, (*STARTS[1:], blocks - 1)))
    width = (blocks + most) * B
    vmem = pl.BlockSpec(memory_space=pltpu.VMEM)
    smem = pl.BlockSpec(memory_space=pltpu.SMEM)
    return pl.pallas_call(
        solve_kernel,
        out_shape=jax.ShapeDtypeStruct((own, queries.shape[0]), jnp.float32),
        in_specs=[vmem, smem, smem, vmem, vmem],
        out_specs=vmem,
        scratch_shapes=[
            pltpu.VMEM((width, width), jnp.float32),
            pltpu.VMEM((width, 3 * B), jnp.bfloat16),
            pltpu.VMEM((width, 3 * B), jnp.bfloat16),
        ],
        compiler_params=pltpu.CompilerParams(vmem_limit_bytes=36 * 2**20),
    )(prior, damping, first, slots, queries)


def to_layer(parts, axis):
    length = lax.axis_size(axis)
    me = lax.axis_index(axis)
    total = lax.dynamic_index_in_dim(parts, me, 0, keepdims=False)
    for d in (1, length - 1, *range(2, length - 1)):
        piece = lax.dynamic_index_in_dim(parts, lax.rem(me + d, length), 0, keepdims=False)
        total = total + lax.ppermute(piece, axis, [(i, (i + d) % length) for i in range(length)])
    return total


def gather_pairs(x, axis):
    length = lax.axis_size(axis)
    chips = length // 2
    groups = [[2 * i + c for i in range(chips)] for c in range(2)]
    spread = jnp.broadcast_to(x[None], (chips, *x.shape))
    mine = lax.all_to_all(spread, axis, 0, 0, axis_index_groups=groups, tiled=True)
    theirs = lax.ppermute(mine, axis, [(i, i ^ 1) for i in range(length)])
    first = lax.rem(lax.axis_index(axis), 2) == 0
    pairs = jnp.stack([jnp.where(first, mine, theirs), jnp.where(first, theirs, mine)], axis=1)
    return pairs.reshape(length * x.shape[0], *x.shape[1:])


def sum_of_four(x, axis):
    other = [lax.ppermute(x, axis, [(i, i ^ d) for i in range(4)]) for d in (1, 2, 3)]
    return (x + other[0]) + (other[1] + other[2])


def per_device(
    activations, out_grads, proj_in, proj_out, lengths, example_ids, prior_cov, damping, queries
):
    ex_local = lengths.shape[0]
    seq_len = activations.shape[1] // ex_local
    tokens = activations.shape[1]
    proj_size = KP * KP
    live_mask = (jnp.arange(seq_len, dtype=jnp.int32)[None, :] < lengths[:, None]).astype(
        jnp.float32
    )
    in_parts = jnp.einsum("ltf,lkf->ltk", activations, proj_in, preferred_element_type=jnp.float32)
    out_parts = jnp.einsum("ltf,lkf->ltk", out_grads, proj_out, preferred_element_type=jnp.float32)
    owned = to_layer(jnp.concatenate([in_parts, out_parts], axis=1), "tensor")
    in_rows = owned[:tokens].reshape(ex_local, seq_len, KP) * live_mask[:, :, None]
    out_rows = owned[tokens:].reshape(ex_local, seq_len, KP)
    proj_grads = jnp.einsum(
        "est,esu->etu", out_rows, in_rows, precision=lax.Precision.HIGHEST
    ).reshape(ex_local, proj_size)
    sent = jnp.concatenate([proj_grads, example_ids.astype(jnp.float32)[:, None]], axis=1)
    gathered = gather_pairs(sent, "dp")
    first = (lax.axis_index("dp") * ex_local).astype(jnp.int32)[None]
    layer_scores = scores_of(prior_cov[0], damping, first, gathered, queries[0], ex_local)
    return sum_of_four(layer_scores, "tensor")


def solution(mesh):
    in_specs = (
        P(None, "dp", "tensor"),
        P(None, "dp", "tensor"),
        P(None, None, "tensor"),
        P(None, None, "tensor"),
        P("dp"),
        P("dp"),
        P("tensor", None, None),
        P("tensor"),
        P("tensor", None, None),
    )
    out_specs = P("dp", None)
    return jax.shard_map(
        per_device, mesh=mesh, in_specs=in_specs, out_specs=out_specs, check_vma=False
    )
```

```python
import jax
import jax.numpy as jnp
from jax import lax
from jax.experimental import pallas as pl
from jax.experimental.pallas import tpu as pltpu
from jax.sharding import PartitionSpec as P

KP = 40
B = 128
S = 16
STARTS = (0, 3, 6, 9)


def split(x):
    high = x.astype(jnp.bfloat16)
    low = (x - high.astype(jnp.float32)).astype(jnp.bfloat16)
    return high, low


def down(row):
    return jnp.broadcast_to(row, (8, B))


def block_inverse(block, groups, beside):
    lane = lax.broadcasted_iota(jnp.int32, (8, B), 1)
    sub = lax.broadcasted_iota(jnp.int32, (8, B), 0)
    rows = [block[8 * h : 8 * h + 8] for h in range(16)]

    def columns(piece, first):
        return [jnp.broadcast_to(piece[:, first + m : first + m + 1], (8, B)) for m in range(S)]

    for g in range(groups):
        first = S * g
        here = (2 * g, 2 * g + 1)
        in_pivot = (lane >= first) & (lane < first + S)
        cols = [list(pair) for pair in zip(*(columns(rows[h], first) for h in here))]
        after = (2 * g + 2, 2 * g + 3) if g + 1 < groups else ()
        next_cols = [columns(rows[h], first) for h in after]
        panel = [
            jnp.where(in_pivot, jnp.where(lane - first == sub + 8 * q, 1.0, 0.0), rows[h])
            for q, h in enumerate(here)
        ]
        for j in range(S):
            a, s = j // 8, j % 8
            pivot = cols[j]
            r = down((1.0 / pivot[a])[s : s + 1])
            others = jnp.where(sub == s, 0.0, pivot[a])
            for item in (*cols[j + 1 :], panel):
                scaled = down(item[a][s : s + 1]) * r
                item[a] = jnp.where(sub == s, scaled, item[a]) - others * scaled
                item[1 - a] = item[1 - a] - pivot[1 - a] * scaled
        high, low = split(jnp.concatenate(panel, axis=0))
        both = jnp.concatenate([high, low], axis=1)
        parts = [jnp.zeros((S, 2 * B), jnp.bfloat16)] * (B // S)
        parts[g] = both
        right = jnp.concatenate(parts + parts, axis=0)
        left = jnp.concatenate(split(jnp.concatenate(rows, axis=0)), axis=1)
        change = jnp.dot(left, right, preferred_element_type=jnp.float32)
        change = change[:, :B] + change[:, B:]
        fresh = []
        for h in range(16):
            if h in here:
                fresh.append(panel[h - here[0]])
                continue
            kept = jnp.where(in_pivot, 0.0, rows[h])
            if h in after:
                terms = [
                    c * down(panel[m // 8][m % 8 : m % 8 + 1])
                    for m, c in enumerate(next_cols[h - after[0]])
                ]
                while len(terms) > 1:
                    terms = [x + y for x, y in zip(terms[::2], terms[1::2])]
                fresh.append(kept - terms[0])
            else:
                fresh.append(kept - change[8 * h : 8 * h + 8])
        rows = fresh
        beside(g)
    return jnp.concatenate(rows, axis=0)


def solve_kernel(prior_ref, damp_ref, first_ref, slots_ref, queries_ref, out_ref, held, work, left, terms, sems):
    size = prior_ref.shape[0]
    blocks = pl.cdiv(size, B)
    tail = blocks * B
    examples = slots_ref.shape[0]
    n_query = queries_ref.shape[0]
    n_own = out_ref.shape[0]
    stripes = [slice(k * B, min((k + 1) * B, size)) for k in range(blocks)]
    copies = [
        pltpu.make_async_copy(
            prior_ref.at[here, 0 : here.stop], held.at[here, 0 : here.stop], sems.at[k]
        )
        for k, here in enumerate(stripes)
    ]
    for copy in copies:
        copy.start()
    r = lax.broadcasted_iota(jnp.int32, (B, B), 0)
    c = lax.broadcasted_iota(jnp.int32, (B, B), 1)

    def set_left(rows, x):
        high, low = split(x)
        left[rows, 0:B] = high
        left[rows, B : 2 * B] = high
        left[rows, 2 * B :] = low

    def set_terms(rows, x):
        high, low = split(x)
        terms[rows, 0:B] = high
        terms[rows, B : 2 * B] = low
        terms[rows, 2 * B :] = high

    slots = jnp.concatenate(
        [slots_ref[...], jnp.zeros((examples, tail - slots_ref.shape[1]), jnp.float32)], axis=1
    )
    slots_t = slots.T
    grads = slots[:, :size]
    grads_t = slots_t[:size]
    ids = jnp.broadcast_to(slots_t[size : size + 1].astype(jnp.int32), (B - n_query, examples))
    row = lax.broadcasted_iota(jnp.int32, (B - n_query, examples), 0)
    pick = jnp.where((ids == row + first_ref[0]) & (row < n_own), 1.0, 0.0)
    work[tail : tail + n_query, 0:size] = queries_ref[...]
    work[tail + n_query : tail + B, 0:size] = jnp.dot(
        pick, grads, preferred_element_type=jnp.float32, precision=lax.Precision.HIGHEST
    )
    work[tail : tail + B, size:tail] = jnp.zeros((B, tail - size), jnp.float32)
    work[tail : tail + B, tail : tail + B] = jnp.zeros((B, B), jnp.float32)
    for ref in (left, terms):
        ref[size:, :] = jnp.zeros((ref.shape[0] - size, ref.shape[1]), ref.dtype)
    set_left(slice(0, size), grads_t)
    set_terms(slice(0, size), grads_t * (-1.0 / examples))

    for k, here in enumerate(stripes):
        copies[k].wait()
        stop = (k + 1) * B
        spot = slice(k * B, stop)
        work[here, 0 : here.stop] = held[here, 0 : here.stop].astype(jnp.float32)
        if here.stop < stop:
            work[here.stop : stop, 0:stop] = jnp.zeros((stop - size, stop), jnp.float32)
            work[here, here.stop : stop] = jnp.zeros((size - k * B, stop - size), jnp.float32)
        work[spot, spot] += jnp.where(r == c, jnp.where(r + k * B < size, damp_ref[0], 1.0), 0.0)

    def product(x, y):
        return lax.dot_general(x, y, (((1,), (1,)), ((), ())), preferred_element_type=jnp.float32)

    def step(k, count, groups):
        def at(t, n=1):
            return pl.ds(pl.multiple_of((k + t) * B, B), n * B)

        def beside(g):
            t = 2 * g
            if t < count:
                n = min(2, count - t)
                rows = at(t, count - t)
                work[rows, at(t, n)] -= product(left[rows, :], terms[at(t, n), :])

        block = work[at(0), at(0)] - product(left[at(0), :], terms[at(0), :])
        inverse = block_inverse(block, groups, beside)
        rows = at(1, count - 1)
        set_left(rows, work[rows, at(0)])
        high, low = split(inverse)
        stacked = jnp.concatenate([high, low, high], axis=0)
        set_terms(rows, jnp.dot(left[rows, :], stacked, preferred_element_type=jnp.float32))

    for start, stop in zip(STARTS, (*STARTS[1:], blocks - 1)):

        def body(k, carry, count=blocks + 1 - start):
            step(k, count, B // S)
            return carry

        lax.fori_loop(start, stop, body, 0)
    step(blocks - 1, 2, pl.cdiv(size - (blocks - 1) * B, S))
    last = slice(tail, tail + B)
    result = product(left[last, :], terms[last, :]) - work[last, last]
    out_ref[...] = result[n_query : n_query + n_own, :n_query]


def scores_of(prior, damping, first, slots, queries, own):
    size = prior.shape[0]
    blocks = pl.cdiv(size, B)
    most = max(b - a for a, b in zip(STARTS, (*STARTS[1:], blocks - 1)))
    width = (blocks + most) * B
    vmem = pl.BlockSpec(memory_space=pltpu.VMEM)
    smem = pl.BlockSpec(memory_space=pltpu.SMEM)
    return pl.pallas_call(
        solve_kernel,
        out_shape=jax.ShapeDtypeStruct((own, queries.shape[0]), jnp.float32),
        in_specs=[pl.BlockSpec(memory_space=pl.ANY), smem, smem, vmem, vmem],
        out_specs=vmem,
        scratch_shapes=[
            pltpu.VMEM((size, size), prior.dtype),
            pltpu.VMEM((width, width), jnp.float32),
            pltpu.VMEM((width, 3 * B), jnp.bfloat16),
            pltpu.VMEM((width, 3 * B), jnp.bfloat16),
            pltpu.SemaphoreType.DMA((blocks,)),
        ],
        compiler_params=pltpu.CompilerParams(vmem_limit_bytes=60 * 2**20),
    )(prior, damping, first, slots, queries)


def to_layer(parts, axis):
    length = lax.axis_size(axis)
    me = lax.axis_index(axis)
    total = lax.dynamic_index_in_dim(parts, me, 0, keepdims=False)
    for d in (1, length - 1, *range(2, length - 1)):
        piece = lax.dynamic_index_in_dim(parts, lax.rem(me + d, length), 0, keepdims=False)
        total = total + lax.ppermute(piece, axis, [(i, (i + d) % length) for i in range(length)])
    return total


def gather_pairs(x, axis):
    length = lax.axis_size(axis)
    chips = length // 2
    groups = [[2 * i + c for i in range(chips)] for c in range(2)]
    spread = jnp.broadcast_to(x[None], (chips, *x.shape))
    mine = lax.all_to_all(spread, axis, 0, 0, axis_index_groups=groups, tiled=True)
    theirs = lax.ppermute(mine, axis, [(i, i ^ 1) for i in range(length)])
    first = lax.rem(lax.axis_index(axis), 2) == 0
    pairs = jnp.stack([jnp.where(first, mine, theirs), jnp.where(first, theirs, mine)], axis=1)
    return pairs.reshape(length * x.shape[0], *x.shape[1:])


def sum_of_four(x, axis):
    other = [lax.ppermute(x, axis, [(i, i ^ d) for i in range(4)]) for d in (1, 2, 3)]
    return (x + other[0]) + (other[1] + other[2])


def per_device(
    activations, out_grads, proj_in, proj_out, lengths, example_ids, prior_cov, damping, queries
):
    ex_local = lengths.shape[0]
    seq_len = activations.shape[1] // ex_local
    tokens = activations.shape[1]
    proj_size = KP * KP
    live_mask = (jnp.arange(seq_len, dtype=jnp.int32)[None, :] < lengths[:, None]).astype(
        jnp.float32
    )
    in_parts = jnp.einsum("ltf,lkf->ltk", activations, proj_in, preferred_element_type=jnp.float32)
    out_parts = jnp.einsum("ltf,lkf->ltk", out_grads, proj_out, preferred_element_type=jnp.float32)
    owned = to_layer(jnp.concatenate([in_parts, out_parts], axis=1), "tensor")
    in_rows = owned[:tokens].reshape(ex_local, seq_len, KP) * live_mask[:, :, None]
    out_rows = owned[tokens:].reshape(ex_local, seq_len, KP)
    proj_grads = jnp.einsum(
        "est,esu->etu", out_rows, in_rows, precision=lax.Precision.HIGHEST
    ).reshape(ex_local, proj_size)
    sent = jnp.concatenate([proj_grads, example_ids.astype(jnp.float32)[:, None]], axis=1)
    gathered = gather_pairs(sent, "dp")
    first = (lax.axis_index("dp") * ex_local).astype(jnp.int32)[None]
    layer_scores = scores_of(prior_cov[0], damping, first, gathered, queries[0], ex_local)
    return sum_of_four(layer_scores, "tensor")


def solution(mesh):
    in_specs = (
        P(None, "dp", "tensor"),
        P(None, "dp", "tensor"),
        P(None, None, "tensor"),
        P(None, None, "tensor"),
        P("dp"),
        P("dp"),
        P("tensor", None, None),
        P("tensor"),
        P("tensor", None, None),
    )
    out_specs = P("dp", None)
    return jax.shard_map(
        per_device, mesh=mesh, in_specs=in_specs, out_specs=out_specs, check_vma=False
    )
```

```python
import jax
import jax.numpy as jnp
from jax import lax
from jax.experimental import pallas as pl
from jax.experimental.pallas import tpu as pltpu
from jax.sharding import PartitionSpec as P

KP = 40
B = 128
S = 16
STARTS = (0, 2, 4, 6, 8, 10)


def split(x):
    high = x.astype(jnp.bfloat16)
    low = (x - high.astype(jnp.float32)).astype(jnp.bfloat16)
    return high, low


def down(row):
    return jnp.broadcast_to(row, (8, B))


def block_inverse(block, groups, beside):
    lane = lax.broadcasted_iota(jnp.int32, (8, B), 1)
    sub = lax.broadcasted_iota(jnp.int32, (8, B), 0)
    rows = [block[8 * h : 8 * h + 8] for h in range(16)]

    def columns(piece, first):
        return [jnp.broadcast_to(piece[:, first + m : first + m + 1], (8, B)) for m in range(S)]

    for g in range(groups):
        first = S * g
        here = (2 * g, 2 * g + 1)
        in_pivot = (lane >= first) & (lane < first + S)
        cols = [list(pair) for pair in zip(*(columns(rows[h], first) for h in here))]
        after = (2 * g + 2, 2 * g + 3) if g + 1 < groups else ()
        next_cols = [columns(rows[h], first) for h in after]
        panel = [
            jnp.where(in_pivot, jnp.where(lane - first == sub + 8 * q, 1.0, 0.0), rows[h])
            for q, h in enumerate(here)
        ]
        for j in range(S):
            a, s = j // 8, j % 8
            pivot = cols[j]
            r = down((1.0 / pivot[a])[s : s + 1])
            others = jnp.where(sub == s, 0.0, pivot[a])
            for item in (*cols[j + 1 :], panel):
                scaled = down(item[a][s : s + 1]) * r
                item[a] = jnp.where(sub == s, scaled, item[a]) - others * scaled
                item[1 - a] = item[1 - a] - pivot[1 - a] * scaled
        high, low = split(jnp.concatenate(panel, axis=0))
        both = jnp.concatenate([high, low], axis=1)
        parts = [jnp.zeros((S, 2 * B), jnp.bfloat16)] * (B // S)
        parts[g] = both
        right = jnp.concatenate(parts + parts, axis=0)
        left = jnp.concatenate(split(jnp.concatenate(rows, axis=0)), axis=1)
        change = jnp.dot(left, right, preferred_element_type=jnp.float32)
        change = change[:, :B] + change[:, B:]
        fresh = []
        for h in range(16):
            if h in here:
                fresh.append(panel[h - here[0]])
                continue
            kept = jnp.where(in_pivot, 0.0, rows[h])
            if h in after:
                terms = [
                    c * down(panel[m // 8][m % 8 : m % 8 + 1])
                    for m, c in enumerate(next_cols[h - after[0]])
                ]
                while len(terms) > 1:
                    terms = [x + y for x, y in zip(terms[::2], terms[1::2])]
                fresh.append(kept - terms[0])
            else:
                fresh.append(kept - change[8 * h : 8 * h + 8])
        rows = fresh
        beside(g)
    return jnp.concatenate(rows, axis=0)


def solve_kernel(prior_ref, damp_ref, first_ref, slots_ref, queries_ref, out_ref, work, left, terms):
    size = prior_ref.shape[0]
    blocks = pl.cdiv(size, B)
    tail = blocks * B
    examples = slots_ref.shape[0]
    n_query = queries_ref.shape[0]
    n_own = out_ref.shape[0]
    r = lax.broadcasted_iota(jnp.int32, (B, B), 0)
    c = lax.broadcasted_iota(jnp.int32, (B, B), 1)

    def set_left(rows, x):
        high, low = split(x)
        left[rows, 0:B] = high
        left[rows, B : 2 * B] = high
        left[rows, 2 * B :] = low

    def set_terms(rows, x):
        high, low = split(x)
        terms[rows, 0:B] = high
        terms[rows, B : 2 * B] = low
        terms[rows, 2 * B :] = high

    for k in range(blocks):
        here = slice(k * B, min((k + 1) * B, size))
        work[here, 0 : here.stop] = prior_ref[here, 0 : here.stop].astype(jnp.float32)
        if here.stop < (k + 1) * B:
            work[here.stop : (k + 1) * B, 0 : (k + 1) * B] = jnp.zeros(((k + 1) * B - size, (k + 1) * B), jnp.float32)
            work[here, here.stop : (k + 1) * B] = jnp.zeros((size - k * B, (k + 1) * B - size), jnp.float32)
        spot = slice(k * B, (k + 1) * B)
        work[spot, spot] += jnp.where(r == c, jnp.where(r + k * B < size, damp_ref[0], 1.0), 0.0)
    slots = jnp.concatenate(
        [slots_ref[...], jnp.zeros((examples, tail - slots_ref.shape[1]), jnp.float32)], axis=1
    )
    slots_t = slots.T
    grads = slots[:, :size]
    grads_t = slots_t[:size]
    ids = jnp.broadcast_to(slots_t[size : size + 1].astype(jnp.int32), (B - n_query, examples))
    row = lax.broadcasted_iota(jnp.int32, (B - n_query, examples), 0)
    pick = jnp.where((ids == row + first_ref[0]) & (row < n_own), 1.0, 0.0)
    work[tail : tail + n_query, 0:size] = queries_ref[...]
    work[tail + n_query : tail + B, 0:size] = jnp.dot(
        pick, grads, preferred_element_type=jnp.float32, precision=lax.Precision.HIGHEST
    )
    work[tail : tail + B, size:tail] = jnp.zeros((B, tail - size), jnp.float32)
    work[tail : tail + B, tail : tail + B] = jnp.zeros((B, B), jnp.float32)
    for ref in (left, terms):
        ref[size:, :] = jnp.zeros((ref.shape[0] - size, ref.shape[1]), ref.dtype)
    set_left(slice(0, size), grads_t)
    set_terms(slice(0, size), grads_t * (-1.0 / examples))

    def product(x, y):
        return lax.dot_general(x, y, (((1,), (1,)), ((), ())), preferred_element_type=jnp.float32)

    def step(k, count, groups):
        def at(t, n=1):
            return pl.ds(pl.multiple_of((k + t) * B, B), n * B)

        def beside(g):
            t = 2 * g
            if t < count:
                n = min(2, count - t)
                rows = at(t, count - t)
                work[rows, at(t, n)] -= product(left[rows, :], terms[at(t, n), :])

        block = work[at(0), at(0)] - product(left[at(0), :], terms[at(0), :])
        inverse = block_inverse(block, groups, beside)
        rows = at(1, count - 1)
        set_left(rows, work[rows, at(0)])
        high, low = split(inverse)
        stacked = jnp.concatenate([high, low, high], axis=0)
        set_terms(rows, jnp.dot(left[rows, :], stacked, preferred_element_type=jnp.float32))

    for start, stop in zip(STARTS, (*STARTS[1:], blocks - 1)):

        def body(k, carry, count=blocks + 1 - start):
            step(k, count, B // S)
            return carry

        lax.fori_loop(start, stop, body, 0)
    step(blocks - 1, 2, pl.cdiv(size - (blocks - 1) * B, S))
    last = slice(tail, tail + B)
    result = product(left[last, :], terms[last, :]) - work[last, last]
    out_ref[...] = result[n_query : n_query + n_own, :n_query]


def scores_of(prior, damping, first, slots, queries, own):
    blocks = pl.cdiv(prior.shape[0], B)
    most = max(b - a for a, b in zip(STARTS, (*STARTS[1:], blocks - 1)))
    width = (blocks + most) * B
    vmem = pl.BlockSpec(memory_space=pltpu.VMEM)
    smem = pl.BlockSpec(memory_space=pltpu.SMEM)
    return pl.pallas_call(
        solve_kernel,
        out_shape=jax.ShapeDtypeStruct((own, queries.shape[0]), jnp.float32),
        in_specs=[vmem, smem, smem, vmem, vmem],
        out_specs=vmem,
        scratch_shapes=[
            pltpu.VMEM((width, width), jnp.float32),
            pltpu.VMEM((width, 3 * B), jnp.bfloat16),
            pltpu.VMEM((width, 3 * B), jnp.bfloat16),
        ],
        compiler_params=pltpu.CompilerParams(vmem_limit_bytes=36 * 2**20),
    )(prior, damping, first, slots, queries)


def to_layer(parts, axis):
    length = lax.axis_size(axis)
    me = lax.axis_index(axis)
    total = lax.dynamic_index_in_dim(parts, me, 0, keepdims=False)
    for d in (1, length - 1, *range(2, length - 1)):
        piece = lax.dynamic_index_in_dim(parts, lax.rem(me + d, length), 0, keepdims=False)
        total = total + lax.ppermute(piece, axis, [(i, (i + d) % length) for i in range(length)])
    return total


def gather_pairs(x, axis):
    length = lax.axis_size(axis)
    chips = length // 2
    groups = [[2 * i + c for i in range(chips)] for c in range(2)]
    spread = jnp.broadcast_to(x[None], (chips, *x.shape))
    mine = lax.all_to_all(spread, axis, 0, 0, axis_index_groups=groups, tiled=True)
    theirs = lax.ppermute(mine, axis, [(i, i ^ 1) for i in range(length)])
    first = lax.rem(lax.axis_index(axis), 2) == 0
    pairs = jnp.stack([jnp.where(first, mine, theirs), jnp.where(first, theirs, mine)], axis=1)
    return pairs.reshape(length * x.shape[0], *x.shape[1:])


def sum_of_four(x, axis):
    other = [lax.ppermute(x, axis, [(i, i ^ d) for i in range(4)]) for d in (1, 2, 3)]
    return (x + other[0]) + (other[1] + other[2])


def per_device(
    activations, out_grads, proj_in, proj_out, lengths, example_ids, prior_cov, damping, queries
):
    ex_local = lengths.shape[0]
    seq_len = activations.shape[1] // ex_local
    tokens = activations.shape[1]
    proj_size = KP * KP
    live_mask = (jnp.arange(seq_len, dtype=jnp.int32)[None, :] < lengths[:, None]).astype(
        jnp.float32
    )
    out_parts = jnp.einsum("ltf,lkf->ltk", out_grads, proj_out, preferred_element_type=jnp.float32)
    activations, out_parts = lax.optimization_barrier((activations, out_parts))
    in_parts = jnp.einsum("ltf,lkf->ltk", activations, proj_in, preferred_element_type=jnp.float32)
    owned = to_layer(jnp.concatenate([in_parts, out_parts], axis=1), "tensor")
    in_rows = owned[:tokens].reshape(ex_local, seq_len, KP) * live_mask[:, :, None]
    out_rows = owned[tokens:].reshape(ex_local, seq_len, KP)
    proj_grads = jnp.einsum(
        "est,esu->etu", out_rows, in_rows, precision=lax.Precision.HIGHEST
    ).reshape(ex_local, proj_size)
    sent = jnp.concatenate([proj_grads, example_ids.astype(jnp.float32)[:, None]], axis=1)
    gathered = gather_pairs(sent, "dp")
    first = (lax.axis_index("dp") * ex_local).astype(jnp.int32)[None]
    layer_scores = scores_of(prior_cov[0], damping, first, gathered, queries[0], ex_local)
    return sum_of_four(layer_scores, "tensor")


def solution(mesh):
    in_specs = (
        P(None, "dp", "tensor"),
        P(None, "dp", "tensor"),
        P(None, None, "tensor"),
        P(None, None, "tensor"),
        P("dp"),
        P("dp"),
        P("tensor", None, None),
        P("tensor"),
        P("tensor", None, None),
    )
    out_specs = P("dp", None)
    return jax.shard_map(
        per_device, mesh=mesh, in_specs=in_specs, out_specs=out_specs, check_vma=False
    )
```
